32 devices in a mesh: row: 8 (over z, y), col: 4 (over x, core).
Axes of the slice: x: 2, y: 2, z: 4, core: 2. Of those that a mesh axis runs over, the one named last changes fastest.
Arguments:
- matrix_blocks: bfloat16 [16, 24, 256, 256], P('row', 'col'), may hold values from 0 to 10, as said below
- matrix_rows: int32 [16, 24], P('row', 'col'), may hold values from 0 to 7, as said below
- matrix_counts: int32 [16, 4], P('row', 'col'), may hold values from 0 to 6, as said below
- slab_blocks: bfloat16 [16, 16, 256, 256], P('row', 'col'), may hold values from 0.099609375 to 1
- slab_inner: int32 [16, 16], P('row', 'col'), may hold values from 0 to 15, as said below
- slab_counts: int32 [16], P('row'), may hold values from 8 to 16
Outputs:
- inflated: bfloat16 [16, 32, 256, 256], P('row', 'col')
The draws below stay inside these ranges and needn't reach their ends.
Inputs may be any that keep to these rules, and one draw needn't show every extreme that they name: `matrix_blocks`: entries are positive. `matrix_rows`: the 6 slots of one matrix block column within one index of col name distinct block rows. `matrix_counts`: each row sums to 16; every matrix block column has an index of col where all 6 slots are live. `slab_inner`: the 16 entries of a row are distinct.
All inputs are finite; a program needn't handle non-finite values.
Results may differ from the reference program's by a relative error of at most 0.001.
Values may be sent and summed in bfloat16 or wider, within the bound.
A program may use at most 192 MiB of HBM per device.

```python
import math
import jax
import jax.numpy as jnp
from jax import lax

BS = 256
KB = 16
CAPA = 6
RB_DEV = 8
KW = 16
WB = 16
NBW = 32
N_COL = 4


def draw_matrix_blocks(key, part):
    first, second = jax.random.split(key)
    slots = N_COL * CAPA
    ranges = (jnp.arange(slots) // CAPA).astype(jnp.float32).reshape(1, slots, 1, 1)
    spread = ranges / max(N_COL - 1, 1)
    values = jax.random.uniform(first, (KW, slots, BS, BS), jnp.float32, 0.1, 1.0)
    rising = jnp.sqrt(1.0 + 2.0 * spread)
    row_scale = jnp.exp(jax.random.uniform(second, (KW, slots, BS, 1), jnp.float32, 0.0, math.log(3.2)))
    return (values * row_scale * rising).astype(jnp.bfloat16)


def draw_matrix_rows(key, part):
    starting = jax.random.randint(key, (KW, N_COL, 1), 0, RB_DEV)
    offset = jnp.arange(CAPA, dtype=jnp.int32)[None, None, :]
    placed = (starting + offset) % RB_DEV
    return placed.reshape(KW, N_COL * CAPA).astype(jnp.int32)


def draw_matrix_counts(key, part):
    first, second = jax.random.split(key)
    full_range = jax.random.randint(first, (KW, 1, 1), 0, N_COL)
    scores = jax.random.randint(second, (KW, N_COL, CAPA), 0, 1 << 20)
    sections = jnp.arange(N_COL, dtype=jnp.int32)[None, :, None]
    scores = scores + jnp.where(sections == full_range, 1 << 21, 0)
    flat = scores.reshape(KW, N_COL * CAPA) * (N_COL * CAPA) + jnp.arange(N_COL * CAPA, dtype=jnp.int32)[None, :]
    unused, chosen = jax.lax.top_k(flat, KB)
    owners = chosen // CAPA
    tallies = jnp.sum((owners[:, :, None] == jnp.arange(N_COL, dtype=jnp.int32)[None, None, :]).astype(jnp.int32), axis=1)
    return tallies.astype(jnp.int32)


def permute_one(subkey):
    return jax.random.permutation(subkey, KW)


def draw_slab_inner(key, part):
    subkeys = jax.random.split(key, WB)
    orders = jax.vmap(permute_one)(subkeys)
    return orders[:, :KB].astype(jnp.int32)


def draw_slab_counts(key, part):
    first, second = jax.random.split(key)
    tallies = jax.random.randint(first, (WB,), KB // 2, KB + 1)
    picked = jax.random.randint(second, (), 0, WB)
    return jnp.where(jnp.arange(WB, dtype=jnp.int32) == picked, KB, tallies).astype(jnp.int32)


def shard_levels(rng, extent, shards, low, high):
    loudness = 1.0
    for axis_at, shards_of in shards:
        heights = jax.random.uniform(jax.random.fold_in(jax.random.fold_in(rng, 6), axis_at), (shards_of,), jnp.float32, low / len(shards), high / len(shards))
        loudness = loudness * jnp.repeat(jnp.exp(heights), extent[axis_at] // shards_of).reshape((-1,) + (1,) * (len(extent) - 1 - axis_at))
    return loudness


def setup_inputs(seed: int = 0) -> dict:
    seeds = jax.random.split(jax.random.key(seed), 7)
    matrix_blocks = draw_matrix_blocks(jax.random.fold_in(seeds[6], 71), 0)
    matrix_rows = draw_matrix_rows(jax.random.fold_in(seeds[6], 71), 0)
    matrix_counts = draw_matrix_counts(jax.random.fold_in(seeds[6], 71), 0)
    slab_blocks = jnp.clip(0.099609375 + 0.9003906 * jax.random.uniform(seeds[3], (WB, KB, BS, BS), jnp.float32) ** shard_levels(seeds[3], (WB, KB, BS, BS), ((0, 8), (1, 4)), -0.2, 0.2), 0.099609375, 1.0).astype(jnp.bfloat16)
    slab_inner = draw_slab_inner(jax.random.fold_in(seeds[6], 71), 0)
    slab_counts = draw_slab_counts(jax.random.fold_in(seeds[6], 71), 0)
    return dict(matrix_blocks=matrix_blocks, matrix_rows=matrix_rows, matrix_counts=matrix_counts, slab_blocks=slab_blocks, slab_inner=slab_inner, slab_counts=slab_counts)


def reference(matrix_blocks, matrix_rows, matrix_counts, slab_blocks, slab_inner, slab_counts):
    blocks = matrix_blocks.reshape(KW, N_COL, CAPA, BS, BS)
    block_rows = matrix_rows.reshape(KW, N_COL, CAPA)
    window_index = jnp.arange(RB_DEV, dtype=jnp.int32)
    slot_index = jnp.arange(CAPA, dtype=jnp.int32)
    slab_index = jnp.arange(KB, dtype=jnp.int32)

    def one_column(column):
        inner = slab_inner[column]
        used = slab_index < slab_counts[column]
        right = slab_blocks[column].astype(jnp.float32)

        def one_range(section):
            selected = blocks[inner, section].astype(jnp.float32)
            chosen_rows = block_rows[inner, section]
            chosen_counts = matrix_counts[inner, section]
            active = (slot_index[None, :] < chosen_counts[:, None]) & used[:, None]
            weight = ((chosen_rows[:, :, None] == window_index) & active[:, :, None]).astype(jnp.float32)
            products = jnp.einsum("qtxz,qzy->qtxy", selected, right, precision=lax.Precision.HIGHEST)
            return jnp.einsum("qti,qtxy->ixy", weight, products, precision=lax.Precision.HIGHEST)

        expanded = lax.map(one_range, jnp.arange(N_COL, dtype=jnp.int32))
        squared = expanded * expanded
        sums = jnp.sum(squared, axis=(0, 1, 2))
        factor = (NBW * BS) / sums
        result = (squared * factor[None, None, None, :]).astype(jnp.bfloat16)
        return result.reshape(NBW, BS, BS)

    return lax.map(one_column, jnp.arange(WB, dtype=jnp.int32))
```

```python
import functools

import jax
import jax.numpy as jnp
from jax import lax
from jax.experimental import pallas as pl
from jax.experimental.pallas import tpu as pltpu
from jax.sharding import PartitionSpec as P

RB_DEV = 8
MESH = pl.DeviceIdType.MESH
CHUNKS = 6
PLAIN = CHUNKS - 1
UP, DOWN, SIDE = 0, 1, 2


def gather_kernel(n_row, n_col, a_ref, b_ref, mr_ref, mc_ref, a_all, b_all, mr_all, mc_all,
                  send, recv, b_send, b_recv, mr_send, mr_recv, mc_send, mc_recv, local):
    n_z = n_row // 2
    r = lax.axis_index("row")
    c = lax.axis_index("col")
    z = lax.div(r, 2)
    y = lax.rem(r, 2)
    other = 1 - y

    barrier = pltpu.get_barrier_semaphore()
    for d in range(1, n_row):
        pl.semaphore_signal(barrier, inc=1, device_id={"row": lax.rem(r + d, n_row)}, device_id_type=MESH)
    for d in range(1, n_col):
        pl.semaphore_signal(barrier, inc=1, device_id={"col": lax.rem(c + d, n_col)}, device_id_type=MESH)
    pl.semaphore_wait(barrier, n_row + n_col - 2)

    def chunk(way, rank, ch, own=False):
        target = {UP: r + 2, DOWN: r - 2, SIDE: 2 * z + other}[way]
        src = a_ref.at[ch] if own else a_all.at[rank, ch]
        return pltpu.make_async_remote_copy(
            src_ref=src, dst_ref=a_all.at[rank, ch], send_sem=send.at[way, rank, ch],
            recv_sem=recv.at[rank, ch], device_id={"row": target}, device_id_type=MESH)

    def arrived(rank, ch):
        pltpu.make_async_remote_copy(
            src_ref=a_all.at[rank, ch], dst_ref=a_all.at[rank, ch], send_sem=send.at[SIDE, rank, ch],
            recv_sem=recv.at[rank, ch], device_id={"row": 2 * z + other}, device_id_type=MESH).wait_recv()

    has_up = z < n_z - 1
    has_down = z > 0

    def small(d):
        return pltpu.make_async_remote_copy(
            src_ref=mr_ref, dst_ref=mr_all.at[r], send_sem=mr_send.at[d], recv_sem=mr_recv.at[d],
            device_id={"row": lax.rem(r + d, n_row)}, device_id_type=MESH)

    def slab(d):
        target = {"col": lax.rem(c + d, n_col)}
        return (
            pltpu.make_async_remote_copy(
                src_ref=mc_ref, dst_ref=mc_all.at[c], send_sem=mc_send.at[d], recv_sem=mc_recv.at[d],
                device_id=target, device_id_type=MESH),
            pltpu.make_async_remote_copy(
                src_ref=b_ref, dst_ref=b_all.at[c], send_sem=b_send.at[d], recv_sem=b_recv.at[d],
                device_id=target, device_id_type=MESH),
        )

    for ch in [PLAIN] + list(range(PLAIN)):
        chunk(SIDE, r, ch, True).start()
    for ch in range(CHUNKS):
        @pl.when(has_up)
        def _():
            chunk(UP, r, ch, True).start()

        @pl.when(has_down)
        def _():
            chunk(DOWN, r, ch, True).start()

    for d in range(1, n_row):
        small(d).start()
    for d in range(1, n_col):
        for copy in slab(d):
            copy.start()
    mine = (
        pltpu.make_async_copy(a_ref, a_all.at[r], local.at[0]),
        pltpu.make_async_copy(b_ref, b_all.at[c], local.at[1]),
        pltpu.make_async_copy(mr_ref, mr_all.at[r], local.at[2]),
        pltpu.make_async_copy(mc_ref, mc_all.at[c], local.at[3]),
    )
    for copy in mine:
        copy.start()

    beside = 2 * z + other
    arrived(beside, PLAIN)

    @pl.when(has_up)
    def _():
        chunk(UP, beside, PLAIN).start()

    @pl.when(has_down)
    def _():
        chunk(DOWN, beside, PLAIN).start()

    steps = [(0, ch, True) for ch in range(PLAIN)] + [(0, PLAIN, False), (1, PLAIN, False)]

    def relay(d, carry):
        for flip, ch, cross in steps:
            column = other if flip else y

            @pl.when(z >= d)
            def _():
                rank = 2 * (z - d) + column
                arrived(rank, ch)

                @pl.when(has_up)
                def _():
                    chunk(UP, rank, ch).start()

                if cross:
                    chunk(SIDE, rank, ch).start()

            @pl.when(z + d < n_z)
            def _():
                rank = 2 * (z + d) + column
                arrived(rank, ch)

                @pl.when(has_down)
                def _():
                    chunk(DOWN, rank, ch).start()

                if cross:
                    chunk(SIDE, rank, ch).start()
        return carry

    lax.fori_loop(1, n_z, relay, 0)

    def crossed(q, carry):
        for ch in range(PLAIN):
            arrived(2 * q + other, ch)
        return carry

    lax.fori_loop(0, n_z, crossed, 0)

    for copy in mine:
        copy.wait()
    for d in range(1, n_row):
        small(d).wait()
    for d in range(1, n_col):
        for copy in slab(d):
            copy.wait()

    for ch in range(CHUNKS):
        chunk(SIDE, r, ch, True).wait_send()

        @pl.when(has_up)
        def _():
            chunk(UP, r, ch, True).wait_send()

        @pl.when(has_down)
        def _():
            chunk(DOWN, r, ch, True).wait_send()

    @pl.when(has_up)
    def _():
        chunk(UP, beside, PLAIN).wait_send()

    @pl.when(has_down)
    def _():
        chunk(DOWN, beside, PLAIN).wait_send()

    def drain(d, carry):
        for flip, ch, cross in steps:
            column = other if flip else y

            @pl.when(z >= d)
            def _():
                rank = 2 * (z - d) + column

                @pl.when(has_up)
                def _():
                    chunk(UP, rank, ch).wait_send()

                if cross:
                    chunk(SIDE, rank, ch).wait_send()

            @pl.when(z + d < n_z)
            def _():
                rank = 2 * (z + d) + column

                @pl.when(has_down)
                def _():
                    chunk(DOWN, rank, ch).wait_send()

                if cross:
                    chunk(SIDE, rank, ch).wait_send()
        return carry

    lax.fori_loop(1, n_z, drain, 0)


def product_kernel(columns, capacity, slots, n_col, mr, mc, counts, a_ref, b_ref, sq_ref, sums_ref, where):
    step = pl.program_id(0)
    last = pl.num_programs(0) - 1
    per_rank = a_ref.shape[1] // capacity
    n_k = where.shape[1]

    @pl.when(step == 0)
    def _():
        sq_ref[...] = jnp.zeros_like(sq_ref)
        for j in range(columns):
            def clear(k, carry):
                where[j, k] = -1
                return carry

            lax.fori_loop(0, n_k, clear, 0)

            def place(q, carry):
                where[j, mc[lax.div(q, slots), 0, j * slots + lax.rem(q, slots)]] = q
                return carry

            lax.fori_loop(0, counts[j], place, 0)

    for kk in range(per_rank):
        live = mr[step, 1, kk]
        for j in range(columns):
            q = where[j, step * per_rank + kk]

            @pl.when(q >= 0)
            def _():
                right = b_ref[lax.div(q, slots), j * slots + lax.rem(q, slots)]

                def multiply(t, carry):
                    i = mr[step, 0, kk * capacity + t]
                    sq_ref[j, i] += jnp.dot(a_ref[0, kk * capacity + t], right,
                                            preferred_element_type=jnp.float32)
                    return carry

                lax.fori_loop(0, live, multiply, 0)

    @pl.when(step == last)
    def _():
        block = sq_ref.shape[2]
        for j in range(columns):
            def square(i, total):
                value = sq_ref[j, i]
                value = value * value
                sq_ref[j, i] = value
                return total + jnp.sum(value.reshape(block // 8, 8, block), axis=0)

            total = lax.fori_loop(0, RB_DEV, square, jnp.zeros((8, block), jnp.float32))
            sums_ref[j] = total


def on_device(n_row, n_col, matrix_blocks, matrix_rows, matrix_counts, slab_blocks, slab_inner, slab_counts):
    per_rank, capacity, block = matrix_blocks.shape[0], matrix_blocks.shape[1], matrix_blocks.shape[2]
    columns, slots = slab_blocks.shape[0], slab_blocks.shape[1]
    held = per_rank * capacity
    size = held // CHUNKS
    a = matrix_blocks.reshape(CHUNKS, size, block, block)
    b = slab_blocks.reshape(columns * slots, block, block)
    mr = jnp.zeros((8, 128), jnp.int32)
    mr = mr.at[0, :held].set(matrix_rows.reshape(held)).at[1, :per_rank].set(matrix_counts.reshape(per_rank))
    mc = jnp.zeros((8, 128), jnp.int32).at[0, :columns * slots].set(slab_inner.reshape(columns * slots))

    hbm = pl.BlockSpec(memory_space=pl.ANY)
    dma = pltpu.SemaphoreType.DMA
    a_all, b_all, mr_all, mc_all = pl.pallas_call(
        functools.partial(gather_kernel, n_row, n_col),
        out_shape=(
            jax.ShapeDtypeStruct((n_row,) + a.shape, a.dtype),
            jax.ShapeDtypeStruct((n_col,) + b.shape, b.dtype),
            jax.ShapeDtypeStruct((n_row, 8, 128), jnp.int32),
            jax.ShapeDtypeStruct((n_col, 8, 128), jnp.int32),
        ),
        in_specs=[hbm] * 4,
        out_specs=(hbm,) * 4,
        scratch_shapes=[
            dma((3, n_row, CHUNKS)), dma((n_row, CHUNKS)),
            dma((n_col,)), dma((n_col,)), dma((n_row,)), dma((n_row,)), dma((n_col,)), dma((n_col,)),
            dma((4,)),
        ],
        compiler_params=pltpu.CompilerParams(collective_id=0, has_side_effects=True),
        name="gather_blocks",
    )(a, b, mr, mc)
    a_all = a_all.reshape(n_row, held, block, block)

    squared, partial = pl.pallas_call(
        functools.partial(product_kernel, columns, capacity, slots, n_col),
        out_shape=(
            jax.ShapeDtypeStruct((columns, RB_DEV, block, block), jnp.float32),
            jax.ShapeDtypeStruct((columns, 8, block), jnp.float32),
        ),
        grid_spec=pltpu.PrefetchScalarGridSpec(
            num_scalar_prefetch=3,
            grid=(n_row,),
            in_specs=[
                pl.BlockSpec((1, held, block, block), lambda s, *_: (s, 0, 0, 0)),
                pl.BlockSpec((n_col, columns * slots, block, block), lambda s, *_: (0, 0, 0, 0)),
            ],
            out_specs=(
                pl.BlockSpec((columns, RB_DEV, block, block), lambda s, *_: (0, 0, 0, 0)),
                pl.BlockSpec((columns, 8, block), lambda s, *_: (0, 0, 0)),
            ),
            scratch_shapes=[pltpu.SMEM((columns, n_row * per_rank), jnp.int32)],
        ),
        compiler_params=pltpu.CompilerParams(vmem_limit_bytes=40 << 20),
        name="block_products",
    )(mr_all, mc_all, slab_counts, a_all, b_all)
    total_rows = float(RB_DEV * n_col * block)
    sums = lax.psum(jnp.sum(partial, axis=1), "col")
    factor = total_rows / sums
    return (squared * factor[:, None, None, :]).astype(jnp.bfloat16)


def solution(mesh):
    return jax.shard_map(
        functools.partial(on_device, mesh.shape["row"], mesh.shape["col"]),
        mesh=mesh,
        in_specs=(
            P("row", "col", None, None),
            P("row", "col"),
            P("row", "col"),
            P("row", "col", None, None),
            P("row", "col"),
            P("row"),
        ),
        out_specs=P("row", "col", None, None),
        check_vma=False,
    )
```

```python
import functools

import jax
import jax.numpy as jnp
from jax import lax
from jax.experimental import pallas as pl
from jax.experimental.pallas import tpu as pltpu
from jax.sharding import PartitionSpec as P

RB_DEV = 8
MESH = pl.DeviceIdType.MESH
CHUNKS = 6
PLAIN = CHUNKS - 1
UP, DOWN, SIDE = 0, 1, 2


def step_kernel(n_row, n_col, shape, a_ref, b_ref, rows_ref, counts_ref, inner_ref, slab_counts, out_ref,
                a_all, b_all, rows_all, counts_all, inner_all, rows_s, counts_s, inner_s,
                stage, dense, right, acc, sums_all,
                send, recv, b_send, b_recv, m_send, m_recv, s_send, s_recv, local):
    columns, slots, per_rank, capacity, block = shape
    n_z = n_row // 2
    r = lax.axis_index("row")
    c = lax.axis_index("col")
    z = lax.div(r, 2)
    y = lax.rem(r, 2)
    other = 1 - y
    beside = 2 * z + other
    has_up = z < n_z - 1
    has_down = z > 0

    barrier = pltpu.get_barrier_semaphore()
    for d in range(1, n_row):
        pl.semaphore_signal(barrier, inc=1, device_id={"row": lax.rem(r + d, n_row)}, device_id_type=MESH)
    for d in range(1, n_col):
        pl.semaphore_signal(barrier, inc=1, device_id={"col": lax.rem(c + d, n_col)}, device_id_type=MESH)
    pl.semaphore_wait(barrier, n_row + n_col - 2)

    def chunk(way, rank, ch, own=False):
        target = {UP: r + 2, DOWN: r - 2, SIDE: beside}[way]
        src = a_ref.at[ch] if own else a_all.at[rank, ch]
        return pltpu.make_async_remote_copy(
            src_ref=src, dst_ref=a_all.at[rank, ch], send_sem=send.at[way, rank, ch],
            recv_sem=recv.at[rank, ch], device_id={"row": target}, device_id_type=MESH)

    def arrived(rank, ch):
        pltpu.make_async_remote_copy(
            src_ref=a_all.at[rank, ch], dst_ref=a_all.at[rank, ch], send_sem=send.at[SIDE, rank, ch],
            recv_sem=recv.at[rank, ch], device_id={"row": beside}, device_id_type=MESH).wait_recv()

    def small(d):
        target = {"row": lax.rem(r + d, n_row)}
        return [
            pltpu.make_async_remote_copy(
                src_ref=src, dst_ref=dst.at[r], send_sem=m_send.at[n, d], recv_sem=m_recv.at[n, d],
                device_id=target, device_id_type=MESH)
            for n, (src, dst) in enumerate(((rows_ref, rows_all), (counts_ref, counts_all)))
        ]

    def slab(d):
        target = {"col": lax.rem(c + d, n_col)}
        return [
            pltpu.make_async_remote_copy(
                src_ref=inner_ref, dst_ref=inner_all.at[c], send_sem=b_send.at[1, d], recv_sem=b_recv.at[1, d],
                device_id=target, device_id_type=MESH),
            pltpu.make_async_remote_copy(
                src_ref=b_ref, dst_ref=b_all.at[c], send_sem=b_send.at[0, d], recv_sem=b_recv.at[0, d],
                device_id=target, device_id_type=MESH),
        ]

    def share(d):
        return pltpu.make_async_remote_copy(
            src_ref=sums_all.at[c], dst_ref=sums_all.at[c], send_sem=s_send.at[d], recv_sem=s_recv.at[d],
            device_id={"col": lax.rem(c + d, n_col)}, device_id_type=MESH)

    for ch in [PLAIN] + list(range(PLAIN)):
        chunk(SIDE, r, ch, True).start()
    for ch in range(CHUNKS):
        @pl.when(has_up)
        def _():
            chunk(UP, r, ch, True).start()

        @pl.when(has_down)
        def _():
            chunk(DOWN, r, ch, True).start()

    for d in range(1, n_row):
        for copy in small(d):
            copy.start()
    for d in range(1, n_col):
        for copy in slab(d):
            copy.start()
    mine = (
        pltpu.make_async_copy(a_ref, a_all.at[r], local.at[0]),
        pltpu.make_async_copy(b_ref, b_all.at[c], local.at[1]),
    )
    for copy in mine:
        copy.start()
    rows_all[r] = rows_ref[...]
    counts_all[r] = counts_ref[...]
    inner_all[c] = inner_ref[...]
    acc[...] = jnp.zeros_like(acc)

    arrived(beside, PLAIN)

    @pl.when(has_up)
    def _():
        chunk(UP, beside, PLAIN).start()

    @pl.when(has_down)
    def _():
        chunk(DOWN, beside, PLAIN).start()

    steps = [(0, ch, True) for ch in range(PLAIN)] + [(0, PLAIN, False), (1, PLAIN, False)]

    def relay(d):
        for flip, ch, cross in steps:
            column = other if flip else y

            @pl.when(z >= d)
            def _():
                rank = 2 * (z - d) + column
                arrived(rank, ch)

                @pl.when(has_up)
                def _():
                    chunk(UP, rank, ch).start()

                if cross:
                    chunk(SIDE, rank, ch).start()

            @pl.when(z + d < n_z)
            def _():
                rank = 2 * (z + d) + column
                arrived(rank, ch)

                @pl.when(has_down)
                def _():
                    chunk(DOWN, rank, ch).start()

                if cross:
                    chunk(SIDE, rank, ch).start()

    def multiply(rank):
        copy = pltpu.make_async_copy(a_all.at[rank], stage, local.at[2])
        copy.start()
        for kk in range(per_rank):
            k = rank * per_rank + kk
            for j in range(columns):
                q = jnp.int32(-1)
                for s in range(n_col * slots):
                    found = (inner_s[s // slots, j, s % slots] == k) & (s < slab_counts[j])
                    q = jnp.where(found, s, q)
                at = jnp.maximum(q, 0)
                value = b_all[lax.div(at, slots), j * slots + lax.rem(at, slots)]
                right[pl.ds(kk * block, block), pl.ds(j * block, block)] = jnp.where(q >= 0, value, jnp.zeros_like(value))
        copy.wait()

        def block_row(i, carry):
            for kk in range(per_rank):
                t = jnp.int32(-1)
                for s in range(capacity):
                    found = (rows_s[rank, kk, s] == i) & (s < counts_s[rank, kk, 0])
                    t = jnp.where(found, s, t)
                at = jnp.maximum(t, 0) + kk * capacity
                size = stage.shape[1]
                value = stage[lax.div(at, size), lax.rem(at, size)]
                dense[:, pl.ds(kk * block, block)] = jnp.where(t >= 0, value, jnp.zeros_like(value))
            rows = pl.ds(pl.multiple_of(i * block, block), block)
            acc[rows, :] += jnp.dot(dense[...], right[...], preferred_element_type=jnp.float32)
            return carry

        lax.fori_loop(0, RB_DEV, block_row, 0)

    def both(d, column, crossed):
        @pl.when(z >= d)
        def _():
            rank = 2 * (z - d) + column
            if crossed:
                for ch in range(PLAIN):
                    arrived(rank, ch)
            multiply(rank)

        @pl.when(z + d < n_z)
        def _():
            rank = 2 * (z + d) + column
            if crossed:
                for ch in range(PLAIN):
                    arrived(rank, ch)
            multiply(rank)

    relay(1)
    for copy in mine:
        copy.wait()
    for d in range(1, n_row):
        for copy in small(d):
            copy.wait()
    for d in range(1, n_col):
        for copy in slab(d):
            copy.wait()
    for n, (src, dst) in enumerate(((rows_all, rows_s), (counts_all, counts_s), (inner_all, inner_s))):
        copy = pltpu.make_async_copy(src, dst, local.at[3 + n])
        copy.start()
        copy.wait()

    multiply(r)
    for ch in range(PLAIN):
        arrived(beside, ch)
    multiply(beside)

    def later(d, carry):
        relay(d)
        both(d - 1, y, False)
        both(d - 1, other, True)
        return carry

    lax.fori_loop(2, n_z, later, 0)
    both(n_z - 1, y, False)
    both(n_z - 1, other, True)

    def square(i, total):
        rows = pl.ds(pl.multiple_of(i * block, block), block)
        value = acc[rows, :]
        value = value * value
        acc[rows, :] = value
        return total + jnp.sum(value.reshape(block // 8, 8, columns * block), axis=0)

    total = lax.fori_loop(0, RB_DEV, square, jnp.zeros((8, columns * block), jnp.float32))
    sums_all[c] = total
    for d in range(1, n_col):
        share(d).start()

    for ch in range(CHUNKS):
        chunk(SIDE, r, ch, True).wait_send()

        @pl.when(has_up)
        def _():
            chunk(UP, r, ch, True).wait_send()

        @pl.when(has_down)
        def _():
            chunk(DOWN, r, ch, True).wait_send()

    @pl.when(has_up)
    def _():
        chunk(UP, beside, PLAIN).wait_send()

    @pl.when(has_down)
    def _():
        chunk(DOWN, beside, PLAIN).wait_send()

    def drain(d, carry):
        for flip, ch, cross in steps:
            column = other if flip else y

            @pl.when(z >= d)
            def _():
                rank = 2 * (z - d) + column

                @pl.when(has_up)
                def _():
                    chunk(UP, rank, ch).wait_send()

                if cross:
                    chunk(SIDE, rank, ch).wait_send()

            @pl.when(z + d < n_z)
            def _():
                rank = 2 * (z + d) + column

                @pl.when(has_down)
                def _():
                    chunk(DOWN, rank, ch).wait_send()

                if cross:
                    chunk(SIDE, rank, ch).wait_send()
        return carry

    lax.fori_loop(1, n_z, drain, 0)

    for d in range(1, n_col):
        share(d).wait()
    sums = jnp.sum(jnp.sum(sums_all[...], axis=0), axis=0, keepdims=True)
    factor = float(RB_DEV * n_col * block) / sums

    def scale(i, carry):
        rows = pl.ds(pl.multiple_of(i * block, block), block)
        value = (acc[rows, :] * factor).astype(jnp.bfloat16)
        for j in range(columns):
            out_ref[j, i] = value[:, j * block:(j + 1) * block]
        return carry

    lax.fori_loop(0, RB_DEV, scale, 0)


def on_device(n_row, n_col, matrix_blocks, matrix_rows, matrix_counts, slab_blocks, slab_inner, slab_counts):
    per_rank, capacity, block = matrix_blocks.shape[0], matrix_blocks.shape[1], matrix_blocks.shape[2]
    columns, slots = slab_blocks.shape[0], slab_blocks.shape[1]
    held = per_rank * capacity
    size = held // CHUNKS
    a = matrix_blocks.reshape(CHUNKS, size, block, block)
    b = slab_blocks.reshape(columns * slots, block, block)
    hbm = pl.BlockSpec(memory_space=pl.ANY)
    vmem = pl.BlockSpec(memory_space=pltpu.VMEM)
    dma = pltpu.SemaphoreType.DMA
    rows_shape, counts_shape, inner_shape = (
        (n_row,) + matrix_rows.shape, (n_row,) + matrix_counts.shape, (n_col,) + slab_inner.shape)
    return pl.pallas_call(
        functools.partial(step_kernel, n_row, n_col, (columns, slots, per_rank, capacity, block)),
        out_shape=jax.ShapeDtypeStruct((columns, RB_DEV, block, block), jnp.bfloat16),
        in_specs=[hbm, hbm, vmem, vmem, vmem, pl.BlockSpec(memory_space=pltpu.SMEM)],
        out_specs=vmem,
        scratch_shapes=[
            pltpu.VMEM((n_row,) + a.shape, a.dtype),
            pltpu.VMEM((n_col,) + b.shape, b.dtype),
            pltpu.VMEM(rows_shape, jnp.int32),
            pltpu.VMEM(counts_shape, jnp.int32),
            pltpu.VMEM(inner_shape, jnp.int32),
            pltpu.SMEM(rows_shape, jnp.int32),
            pltpu.SMEM(counts_shape, jnp.int32),
            pltpu.SMEM(inner_shape, jnp.int32),
            pltpu.VMEM(a.shape, a.dtype),
            pltpu.VMEM((block, per_rank * block), a.dtype),
            pltpu.VMEM((per_rank * block, columns * block), b.dtype),
            pltpu.VMEM((RB_DEV * block, columns * block), jnp.float32),
            pltpu.VMEM((n_col, 8, columns * block), jnp.float32),
            dma((3, n_row, CHUNKS)), dma((n_row, CHUNKS)),
            dma((2, n_col)), dma((2, n_col)), dma((2, n_row)), dma((2, n_row)), dma((n_col,)), dma((n_col,)),
            dma((6,)),
        ],
        compiler_params=pltpu.CompilerParams(
            collective_id=0, has_side_effects=True, vmem_limit_bytes=52 << 20),
        name="gather_multiply_normalize",
    )(a, b, matrix_rows, matrix_counts, slab_inner, slab_counts)


def solution(mesh):
    return jax.shard_map(
        functools.partial(on_device, mesh.shape["row"], mesh.shape["col"]),
        mesh=mesh,
        in_specs=(
            P("row", "col", None, None),
            P("row", "col"),
            P("row", "col"),
            P("row", "col", None, None),
            P("row", "col"),
            P("row"),
        ),
        out_specs=P("row", "col", None, None),
        check_vma=False,
    )
```

```python
import functools

import jax
import jax.numpy as jnp
from jax import lax
from jax.experimental import pallas as pl
from jax.experimental.pallas import tpu as pltpu
from jax.sharding import PartitionSpec as P

RB_DEV = 8
MESH = pl.DeviceIdType.MESH
CHUNKS = 6
PLAIN = CHUNKS - 1
UP, DOWN, SIDE = 0, 1, 2


def step_kernel(n_row, n_col, shape, a_ref, b_ref, rows_ref, counts_ref, inner_ref, slab_counts, out_ref,
                a_all, b_all, rows_all, counts_all, inner_all, rows_s, counts_s, inner_s,
                slot_s, source_s, stage, right, acc, sums_all,
                send, recv, b_send, b_recv, m_send, m_recv, s_send, s_recv, local):
    columns, slots, per_rank, capacity, block = shape
    each = CHUNKS // per_rank
    size = capacity // each
    n_z = n_row // 2
    r = lax.axis_index("row")
    c = lax.axis_index("col")
    z = lax.div(r, 2)
    y = lax.rem(r, 2)
    other = 1 - y
    beside = 2 * z + other
    has_up = z < n_z - 1
    has_down = z > 0

    barrier = pltpu.get_barrier_semaphore()
    for d in range(1, n_row):
        pl.semaphore_signal(barrier, inc=1, device_id={"row": lax.rem(r + d, n_row)}, device_id_type=MESH)
    for d in range(1, n_col):
        pl.semaphore_signal(barrier, inc=1, device_id={"col": lax.rem(c + d, n_col)}, device_id_type=MESH)
    pl.semaphore_wait(barrier, n_row + n_col - 2)

    def chunk(way, rank, ch, own=False):
        target = {UP: r + 2, DOWN: r - 2, SIDE: beside}[way]
        src = a_ref.at[ch] if own else a_all.at[rank, ch]
        return pltpu.make_async_remote_copy(
            src_ref=src, dst_ref=a_all.at[rank, ch], send_sem=send.at[way, rank, ch],
            recv_sem=recv.at[rank, ch], device_id={"row": target}, device_id_type=MESH)

    def arrived(rank, ch):
        pltpu.make_async_remote_copy(
            src_ref=a_all.at[rank, ch], dst_ref=a_all.at[rank, ch], send_sem=send.at[SIDE, rank, ch],
            recv_sem=recv.at[rank, ch], device_id={"row": beside}, device_id_type=MESH).wait_recv()

    def small(d):
        target = {"row": lax.rem(r + d, n_row)}
        return [
            pltpu.make_async_remote_copy(
                src_ref=src, dst_ref=dst.at[r], send_sem=m_send.at[n, d], recv_sem=m_recv.at[n, d],
                device_id=target, device_id_type=MESH)
            for n, (src, dst) in enumerate(((rows_ref, rows_all), (counts_ref, counts_all)))
        ]

    def slab(d):
        target = {"col": lax.rem(c + d, n_col)}
        return [
            pltpu.make_async_remote_copy(
                src_ref=inner_ref, dst_ref=inner_all.at[c], send_sem=b_send.at[1, d], recv_sem=b_recv.at[1, d],
                device_id=target, device_id_type=MESH),
            pltpu.make_async_remote_copy(
                src_ref=b_ref, dst_ref=b_all.at[c], send_sem=b_send.at[0, d], recv_sem=b_recv.at[0, d],
                device_id=target, device_id_type=MESH),
        ]

    def share(d):
        return pltpu.make_async_remote_copy(
            src_ref=sums_all.at[c], dst_ref=sums_all.at[c], send_sem=s_send.at[d], recv_sem=s_recv.at[d],
            device_id={"col": lax.rem(c + d, n_col)}, device_id_type=MESH)

    for ch in [PLAIN] + list(range(PLAIN)):
        chunk(SIDE, r, ch, True).start()
    for ch in range(CHUNKS):
        @pl.when(has_up)
        def _():
            chunk(UP, r, ch, True).start()

        @pl.when(has_down)
        def _():
            chunk(DOWN, r, ch, True).start()

    for d in range(1, n_row):
        for copy in small(d):
            copy.start()
    for d in range(1, n_col):
        for copy in slab(d):
            copy.start()
    mine = (
        pltpu.make_async_copy(a_ref, a_all.at[r], local.at[0]),
        pltpu.make_async_copy(b_ref, b_all.at[c], local.at[1]),
        pltpu.make_async_copy(rows_ref, rows_all.at[r], local.at[2]),
        pltpu.make_async_copy(counts_ref, counts_all.at[r], local.at[3]),
        pltpu.make_async_copy(inner_ref, inner_all.at[c], local.at[4]),
    )
    for copy in mine:
        copy.start()
    acc[...] = jnp.zeros_like(acc)

    arrived(beside, PLAIN)

    @pl.when(has_up)
    def _():
        chunk(UP, beside, PLAIN).start()

    @pl.when(has_down)
    def _():
        chunk(DOWN, beside, PLAIN).start()

    steps = [(0, ch, True) for ch in range(PLAIN)] + [(0, PLAIN, False), (1, PLAIN, False)]

    def sides(d, work):
        def one(side, carry):
            at = z + d * (2 * side - 1)

            @pl.when((at >= 0) & (at < n_z))
            def _():
                work(at)
            return carry

        lax.fori_loop(0, 2, one, 0)

    def relay(d, extra):
        for n, (flip, ch, cross) in enumerate(steps):
            column = other if flip else y

            @pl.when(z >= d)
            def _():
                rank = 2 * (z - d) + column
                arrived(rank, ch)

                @pl.when(has_up)
                def _():
                    chunk(UP, rank, ch).start()

                if cross:
                    chunk(SIDE, rank, ch).start()

            @pl.when(z + d < n_z)
            def _():
                rank = 2 * (z + d) + column
                arrived(rank, ch)

                @pl.when(has_down)
                def _():
                    chunk(DOWN, rank, ch).start()

                if cross:
                    chunk(SIDE, rank, ch).start()

            for work in extra.get(n, ()):
                work()

    def half(rank, kk):
        k = rank * per_rank + kk
        copy = pltpu.make_async_copy(a_all.at[rank, pl.ds(kk * each, each)], stage, local.at[0])
        copy.start()
        for j in range(columns):
            q = source_s[k, j]
            at = jnp.maximum(q, 0)
            value = b_all[lax.div(at, slots), j * slots + lax.rem(at, slots)]
            right[:, j * block:(j + 1) * block] = jnp.where(q >= 0, value, jnp.zeros_like(value))
        copy.wait()

        def block_row(i, carry):
            t = slot_s[k, i]
            at = jnp.maximum(t, 0)
            value = stage[lax.div(at, size), lax.rem(at, size)]
            left = jnp.where(t >= 0, value, jnp.zeros_like(value))
            rows = pl.ds(pl.multiple_of(i * block, block), block)
            acc[rows, :] += jnp.dot(left, right[...], preferred_element_type=jnp.float32)
            return carry

        lax.fori_loop(0, RB_DEV, block_row, 0, unroll=2)

    def whole(rank):
        def one(kk, carry):
            half(rank, kk)
            return carry

        lax.fori_loop(0, per_rank, one, 0)

    def await_side(rank, first, end):
        for ch in range(first, end):
            arrived(rank, ch)

    def own_whole(at):
        whole(2 * at + y)

    def side_whole(at):
        await_side(2 * at + other, 0, PLAIN)
        whole(2 * at + other)

    def own_half(kk):
        def work(at):
            half(2 * at + y, kk)
        return work

    def side_half(kk):
        def work(at):
            await_side(2 * at + other, kk * each, min(kk * each + each, PLAIN))
            half(2 * at + other, kk)
        return work

    relay(1, {})
    for copy in mine:
        copy.wait()
    for d in range(1, n_row):
        for copy in small(d):
            copy.wait()
    for d in range(1, n_col):
        for copy in slab(d):
            copy.wait()
    for n, (src, dst) in enumerate(((rows_all, rows_s), (counts_all, counts_s), (inner_all, inner_s))):
        copy = pltpu.make_async_copy(src, dst, local.at[5 + n])
        copy.start()
        copy.wait()

    def table(rank, carry):
        for kk in range(per_rank):
            k = rank * per_rank + kk
            for j in range(columns):
                q = jnp.int32(-1)
                for n in range(n_col * slots):
                    found = (inner_s[n // slots, j, n % slots] == k) & (n < slab_counts[j])
                    q = jnp.where(found, n, q)
                source_s[k, j] = q
            for i in range(RB_DEV):
                t = jnp.int32(-1)
                for n in range(capacity):
                    found = (rows_s[rank, kk, n] == i) & (n < counts_s[rank, kk, 0])
                    t = jnp.where(found, n, t)
                slot_s[k, i] = t
        return carry

    lax.fori_loop(0, n_row, table, 0)
    await_side(beside, 0, PLAIN)

    def here(column, carry):
        whole(2 * z + column)
        return carry

    lax.fori_loop(0, 2, here, 0)
    sides(1, own_whole)

    def later(d, carry):
        relay(d, {})
        sides(d - 1, side_whole)
        sides(d, own_whole)
        return carry

    lax.fori_loop(2, n_z - 1, later, 0)
    far = n_z - 1
    relay(far, {
        each - 1: (lambda: sides(far, own_half(0)), lambda: sides(far - 1, side_whole)),
        CHUNKS - 1: (lambda: sides(far, own_half(1)), lambda: sides(far, side_half(0))),
        CHUNKS: (lambda: sides(far, side_half(1)),),
    })

    def square(i, total):
        rows = pl.ds(pl.multiple_of(i * block, block), block)
        value = acc[rows, :]
        value = value * value
        return total + jnp.sum(value.reshape(block // 8, 8, columns * block), axis=0)

    total = lax.fori_loop(0, RB_DEV, square, jnp.zeros((8, columns * block), jnp.float32))
    sums_all[c] = total
    for d in range(1, n_col):
        share(d).start()

    for ch in range(CHUNKS):
        chunk(SIDE, r, ch, True).wait_send()

        @pl.when(has_up)
        def _():
            chunk(UP, r, ch, True).wait_send()

        @pl.when(has_down)
        def _():
            chunk(DOWN, r, ch, True).wait_send()

    @pl.when(has_up)
    def _():
        chunk(UP, beside, PLAIN).wait_send()

    @pl.when(has_down)
    def _():
        chunk(DOWN, beside, PLAIN).wait_send()

    def drain(d, carry):
        for flip, ch, cross in steps:
            column = other if flip else y

            @pl.when(z >= d)
            def _():
                rank = 2 * (z - d) + column

                @pl.when(has_up)
                def _():
                    chunk(UP, rank, ch).wait_send()

                if cross:
                    chunk(SIDE, rank, ch).wait_send()

            @pl.when(z + d < n_z)
            def _():
                rank = 2 * (z + d) + column

                @pl.when(has_down)
                def _():
                    chunk(DOWN, rank, ch).wait_send()

                if cross:
                    chunk(SIDE, rank, ch).wait_send()
        return carry

    lax.fori_loop(1, n_z, drain, 0)

    for d in range(1, n_col):
        share(d).wait()
    sums = jnp.sum(jnp.sum(sums_all[...], axis=0), axis=0, keepdims=True)
    factor = float(RB_DEV * n_col * block) / sums

    def scale(i, carry):
        rows = pl.ds(pl.multiple_of(i * block, block), block)
        value = acc[rows, :]
        value = (value * value * factor).astype(jnp.bfloat16)
        for j in range(columns):
            out_ref[j, i] = value[:, j * block:(j + 1) * block]
        return carry

    lax.fori_loop(0, RB_DEV, scale, 0)


def on_device(n_row, n_col, matrix_blocks, matrix_rows, matrix_counts, slab_blocks, slab_inner, slab_counts):
    per_rank, capacity, block = matrix_blocks.shape[0], matrix_blocks.shape[1], matrix_blocks.shape[2]
    columns, slots = slab_blocks.shape[0], slab_blocks.shape[1]
    held = per_rank * capacity
    size = held // CHUNKS
    a = matrix_blocks.reshape(CHUNKS, size, block, block)
    b = slab_blocks.reshape(columns * slots, block, block)
    hbm = pl.BlockSpec(memory_space=pltpu.HBM)
    vmem = pl.BlockSpec(memory_space=pltpu.VMEM)
    dma = pltpu.SemaphoreType.DMA
    rows_shape, counts_shape, inner_shape = (
        (n_row,) + matrix_rows.shape, (n_row,) + matrix_counts.shape, (n_col,) + slab_inner.shape)
    return pl.pallas_call(
        functools.partial(step_kernel, n_row, n_col, (columns, slots, per_rank, capacity, block)),
        out_shape=jax.ShapeDtypeStruct((columns, RB_DEV, block, block), jnp.bfloat16),
        in_specs=[hbm, hbm, hbm, hbm, hbm, pl.BlockSpec(memory_space=pltpu.SMEM)],
        out_specs=vmem,
        scratch_shapes=[
            pltpu.VMEM((n_row,) + a.shape, a.dtype),
            pltpu.VMEM((n_col,) + b.shape, b.dtype),
            pltpu.VMEM(rows_shape, jnp.int32),
            pltpu.VMEM(counts_shape, jnp.int32),
            pltpu.VMEM(inner_shape, jnp.int32),
            pltpu.SMEM(rows_shape, jnp.int32),
            pltpu.SMEM(counts_shape, jnp.int32),
            pltpu.SMEM(inner_shape, jnp.int32),
            pltpu.SMEM((n_row * per_rank, RB_DEV), jnp.int32),
            pltpu.SMEM((n_row * per_rank, columns), jnp.int32),
            pltpu.VMEM((CHUNKS // per_rank, size, block, block), a.dtype),
            pltpu.VMEM((block, columns * block), b.dtype),
            pltpu.VMEM((RB_DEV * block, columns * block), jnp.float32),
            pltpu.VMEM((n_col, 8, columns * block), jnp.float32),
            dma((3, n_row, CHUNKS)), dma((n_row, CHUNKS)),
            dma((2, n_col)), dma((2, n_col)), dma((2, n_row)), dma((2, n_row)), dma((n_col,)), dma((n_col,)),
            dma((8,)),
        ],
        compiler_params=pltpu.CompilerParams(
            collective_id=0, has_side_effects=True, vmem_limit_bytes=63 << 20),
        name="gather_multiply_normalize",
    )(a, b, matrix_rows, matrix_counts, slab_inner, slab_counts)


def solution(mesh):
    return jax.shard_map(
        functools.partial(on_device, mesh.shape["row"], mesh.shape["col"]),
        mesh=mesh,
        in_specs=(
            P("row", "col", None, None),
            P("row", "col"),
            P("row", "col"),
            P("row", "col", None, None),
            P("row", "col"),
            P("row"),
        ),
        out_specs=P("row", "col", None, None),
        check_vma=False,
    )
```

```python
import functools

import jax
import jax.numpy as jnp
from jax import lax
from jax.experimental import pallas as pl
from jax.experimental.pallas import tpu as pltpu
from jax.sharding import PartitionSpec as P

RB_DEV = 8
MESH = pl.DeviceIdType.MESH
CHUNKS = 6
PLAIN = CHUNKS - 1
UP, DOWN, SIDE = 0, 1, 2


def step_kernel(n_row, n_col, shape, a_ref, b_ref, rows_ref, counts_ref, inner_ref, slab_counts, out_ref,
                a_all, b_all, rows_all, counts_all, inner_all, rows_s, counts_s, inner_s,
                slot_s, source_s, stage, right, acc, sums_all, result,
                send, recv, b_send, b_recv, m_send, m_recv, s_send, s_recv, local, done):
    columns, slots, per_rank, capacity, block = shape
    each = CHUNKS // per_rank
    size = capacity // each
    n_z = n_row // 2
    r = lax.axis_index("row")
    c = lax.axis_index("col")
    z = lax.div(r, 2)
    y = lax.rem(r, 2)
    other = 1 - y
    beside = 2 * z + other
    has_up = z < n_z - 1
    has_down = z > 0

    barrier = pltpu.get_barrier_semaphore()
    for d in range(1, n_row):
        pl.semaphore_signal(barrier, inc=1, device_id={"row": lax.rem(r + d, n_row)}, device_id_type=MESH)
    for d in range(1, n_col):
        pl.semaphore_signal(barrier, inc=1, device_id={"col": lax.rem(c + d, n_col)}, device_id_type=MESH)
    pl.semaphore_wait(barrier, n_row + n_col - 2)

    def chunk(way, rank, ch, own=False):
        target = {UP: r + 2, DOWN: r - 2, SIDE: beside}[way]
        src = a_ref.at[ch] if own else a_all.at[rank, ch]
        return pltpu.make_async_remote_copy(
            src_ref=src, dst_ref=a_all.at[rank, ch], send_sem=send.at[way, rank, ch],
            recv_sem=recv.at[rank, ch], device_id={"row": target}, device_id_type=MESH)

    def arrived(rank, ch):
        pltpu.make_async_remote_copy(
            src_ref=a_all.at[rank, ch], dst_ref=a_all.at[rank, ch], send_sem=send.at[SIDE, rank, ch],
            recv_sem=recv.at[rank, ch], device_id={"row": beside}, device_id_type=MESH).wait_recv()

    def small(d):
        target = {"row": lax.rem(r + d, n_row)}
        return [
            pltpu.make_async_remote_copy(
                src_ref=src, dst_ref=dst.at[r], send_sem=m_send.at[n, d], recv_sem=m_recv.at[n, d],
                device_id=target, device_id_type=MESH)
            for n, (src, dst) in enumerate(((rows_ref, rows_all), (counts_ref, counts_all)))
        ]

    def slab(d):
        target = {"col": lax.rem(c + d, n_col)}
        return [
            pltpu.make_async_remote_copy(
                src_ref=inner_ref, dst_ref=inner_all.at[c], send_sem=b_send.at[1, d], recv_sem=b_recv.at[1, d],
                device_id=target, device_id_type=MESH),
            pltpu.make_async_remote_copy(
                src_ref=b_ref, dst_ref=b_all.at[c], send_sem=b_send.at[0, d], recv_sem=b_recv.at[0, d],
                device_id=target, device_id_type=MESH),
        ]

    def share(d):
        return pltpu.make_async_remote_copy(
            src_ref=sums_all.at[c], dst_ref=sums_all.at[c], send_sem=s_send.at[d], recv_sem=s_recv.at[d],
            device_id={"col": lax.rem(c + d, n_col)}, device_id_type=MESH)

    for ch in [PLAIN] + list(range(PLAIN)):
        chunk(SIDE, r, ch, True).start()
    for ch in range(CHUNKS):
        @pl.when(has_up)
        def _():
            chunk(UP, r, ch, True).start()

        @pl.when(has_down)
        def _():
            chunk(DOWN, r, ch, True).start()

    for d in range(1, n_row):
        for copy in small(d):
            copy.start()
    for d in range(1, n_col):
        for copy in slab(d):
            copy.start()
    mine = (
        pltpu.make_async_copy(a_ref, a_all.at[r], local.at[0]),
        pltpu.make_async_copy(b_ref, b_all.at[c], local.at[1]),
        pltpu.make_async_copy(rows_ref, rows_all.at[r], local.at[2]),
        pltpu.make_async_copy(counts_ref, counts_all.at[r], local.at[3]),
        pltpu.make_async_copy(inner_ref, inner_all.at[c], local.at[4]),
    )
    for copy in mine:
        copy.start()
    acc[...] = jnp.zeros_like(acc)

    arrived(beside, PLAIN)

    @pl.when(has_up)
    def _():
        chunk(UP, beside, PLAIN).start()

    @pl.when(has_down)
    def _():
        chunk(DOWN, beside, PLAIN).start()

    steps = [(0, ch, True) for ch in range(PLAIN)] + [(0, PLAIN, False), (1, PLAIN, False)]

    def sides(d, work):
        def one(side, carry):
            at = z + d * (2 * side - 1)

            @pl.when((at >= 0) & (at < n_z))
            def _():
                work(at)
            return carry

        lax.fori_loop(0, 2, one, 0)

    def relay(d, extra):
        for n, (flip, ch, cross) in enumerate(steps):
            column = other if flip else y

            @pl.when(z >= d)
            def _():
                rank = 2 * (z - d) + column
                arrived(rank, ch)

                @pl.when(has_up)
                def _():
                    chunk(UP, rank, ch).start()

                if cross:
                    chunk(SIDE, rank, ch).start()

            @pl.when(z + d < n_z)
            def _():
                rank = 2 * (z + d) + column
                arrived(rank, ch)

                @pl.when(has_down)
                def _():
                    chunk(DOWN, rank, ch).start()

                if cross:
                    chunk(SIDE, rank, ch).start()

            for work in extra.get(n, ()):
                work()

    def half(rank, kk):
        k = rank * per_rank + kk
        copy = pltpu.make_async_copy(a_all.at[rank, pl.ds(kk * each, each)], stage, local.at[0])
        copy.start()
        for j in range(columns):
            q = source_s[k, j]
            at = jnp.maximum(q, 0)
            value = b_all[lax.div(at, slots), j * slots + lax.rem(at, slots)]
            right[:, j * block:(j + 1) * block] = jnp.where(q >= 0, value, jnp.zeros_like(value))
        copy.wait()

        def block_row(i, carry):
            t = slot_s[k, i]
            at = jnp.maximum(t, 0)
            value = stage[lax.div(at, size), lax.rem(at, size)]
            left = jnp.where(t >= 0, value, jnp.zeros_like(value))
            rows = pl.ds(pl.multiple_of(i * block, block), block)
            acc[rows, :] += jnp.dot(left, right[...], preferred_element_type=jnp.float32)
            return carry

        lax.fori_loop(0, RB_DEV, block_row, 0, unroll=2)

    def whole(rank):
        def one(kk, carry):
            half(rank, kk)
            return carry

        lax.fori_loop(0, per_rank, one, 0)

    def await_side(rank, first, end):
        for ch in range(first, end):
            arrived(rank, ch)

    def own_whole(at):
        whole(2 * at + y)

    def side_whole(at):
        await_side(2 * at + other, 0, PLAIN)
        whole(2 * at + other)

    def own_half(kk):
        def work(at):
            half(2 * at + y, kk)
        return work

    def side_half(kk):
        def work(at):
            await_side(2 * at + other, kk * each, min(kk * each + each, PLAIN))
            half(2 * at + other, kk)
        return work

    relay(1, {})
    for copy in mine:
        copy.wait()
    for d in range(1, n_row):
        for copy in small(d):
            copy.wait()
    for d in range(1, n_col):
        for copy in slab(d):
            copy.wait()
    for n, (src, dst) in enumerate(((rows_all, rows_s), (counts_all, counts_s), (inner_all, inner_s))):
        copy = pltpu.make_async_copy(src, dst, local.at[5 + n])
        copy.start()
        copy.wait()

    def table(rank, carry):
        for kk in range(per_rank):
            k = rank * per_rank + kk
            for j in range(columns):
                q = jnp.int32(-1)
                for n in range(n_col * slots):
                    found = (inner_s[n // slots, j, n % slots] == k) & (n < slab_counts[j])
                    q = jnp.where(found, n, q)
                source_s[k, j] = q
            for i in range(RB_DEV):
                t = jnp.int32(-1)
                for n in range(capacity):
                    found = (rows_s[rank, kk, n] == i) & (n < counts_s[rank, 0, kk])
                    t = jnp.where(found, n, t)
                slot_s[k, i] = t
        return carry

    lax.fori_loop(0, n_row, table, 0)
    await_side(beside, 0, PLAIN)

    def here(column, carry):
        whole(2 * z + column)
        return carry

    lax.fori_loop(0, 2, here, 0)
    sides(1, own_whole)

    def later(d, carry):
        relay(d, {})
        sides(d - 1, side_whole)
        sides(d, own_whole)
        return carry

    lax.fori_loop(2, n_z - 1, later, 0)
    far = n_z - 1

    def side_halves(at):
        side_half(0)(at)
        side_half(1)(at)

    relay(far, {
        each - 1: (lambda: sides(far, own_half(0)), lambda: sides(far - 1, side_halves)),
        CHUNKS - 1: (lambda: sides(far, own_half(1)), lambda: sides(far, side_half(0))),
        CHUNKS: (lambda: sides(far, side_half(1)),),
    })

    def square(i, total):
        rows = pl.ds(pl.multiple_of(i * block, block), block)
        value = acc[rows, :]
        value = value * value
        return total + jnp.sum(value.reshape(block // 8, 8, columns * block), axis=0)

    total = lax.fori_loop(0, RB_DEV, square, jnp.zeros((8, columns * block), jnp.float32))
    sums_all[c] = total
    for d in range(1, n_col):
        share(d).start()

    for ch in range(CHUNKS):
        chunk(SIDE, r, ch, True).wait_send()

        @pl.when(has_up)
        def _():
            chunk(UP, r, ch, True).wait_send()

        @pl.when(has_down)
        def _():
            chunk(DOWN, r, ch, True).wait_send()

    @pl.when(has_up)
    def _():
        chunk(UP, beside, PLAIN).wait_send()

    @pl.when(has_down)
    def _():
        chunk(DOWN, beside, PLAIN).wait_send()

    def drain(d, carry):
        for flip, ch, cross in steps:
            column = other if flip else y

            @pl.when(z >= d)
            def _():
                rank = 2 * (z - d) + column

                @pl.when(has_up)
                def _():
                    chunk(UP, rank, ch).wait_send()

                if cross:
                    chunk(SIDE, rank, ch).wait_send()

            @pl.when(z + d < n_z)
            def _():
                rank = 2 * (z + d) + column

                @pl.when(has_down)
                def _():
                    chunk(DOWN, rank, ch).wait_send()

                if cross:
                    chunk(SIDE, rank, ch).wait_send()
        return carry

    lax.fori_loop(1, n_z, drain, 0)

    for d in range(1, n_col):
        share(d).wait()
    sums = jnp.sum(jnp.sum(sums_all[...], axis=0), axis=0, keepdims=True)
    factor = float(RB_DEV * n_col * block) / sums

    def scale(i, carry):
        rows = pl.ds(pl.multiple_of(i * block, block), block)
        value = acc[rows, :]
        value = (value * value * factor).astype(jnp.bfloat16)
        for j in range(columns):
            result[j, i] = value[:, j * block:(j + 1) * block]
            pltpu.make_async_copy(result.at[j, i], out_ref.at[j, i], done.at[j, i]).start()
        return carry

    lax.fori_loop(0, RB_DEV, scale, 0)

    def finish(i, carry):
        for j in range(columns):
            pltpu.make_async_copy(result.at[j, i], out_ref.at[j, i], done.at[j, i]).wait()
        return carry

    lax.fori_loop(0, RB_DEV, finish, 0)


def on_device(n_row, n_col, matrix_blocks, matrix_rows, matrix_counts, slab_blocks, slab_inner, slab_counts):
    per_rank, capacity, block = matrix_blocks.shape[0], matrix_blocks.shape[1], matrix_blocks.shape[2]
    columns, slots = slab_blocks.shape[0], slab_blocks.shape[1]
    held = per_rank * capacity
    size = held // CHUNKS
    a = matrix_blocks.reshape(CHUNKS, size, block, block)
    b = slab_blocks.reshape(columns * slots, block, block)
    matrix_counts = matrix_counts.reshape(1, per_rank)
    hbm = pl.BlockSpec(memory_space=pltpu.HBM)
    dma = pltpu.SemaphoreType.DMA
    rows_shape, counts_shape, inner_shape = (
        (n_row,) + matrix_rows.shape, (n_row,) + matrix_counts.shape, (n_col,) + slab_inner.shape)
    return pl.pallas_call(
        functools.partial(step_kernel, n_row, n_col, (columns, slots, per_rank, capacity, block)),
        out_shape=jax.ShapeDtypeStruct((columns, RB_DEV, block, block), jnp.bfloat16),
        in_specs=[hbm, hbm, hbm, hbm, hbm, pl.BlockSpec(memory_space=pltpu.SMEM)],
        out_specs=hbm,
        scratch_shapes=[
            pltpu.VMEM((n_row,) + a.shape, a.dtype),
            pltpu.VMEM((n_col,) + b.shape, b.dtype),
            pltpu.VMEM(rows_shape, jnp.int32),
            pltpu.VMEM(counts_shape, jnp.int32),
            pltpu.VMEM(inner_shape, jnp.int32),
            pltpu.SMEM(rows_shape, jnp.int32),
            pltpu.SMEM(counts_shape, jnp.int32),
            pltpu.SMEM(inner_shape, jnp.int32),
            pltpu.SMEM((n_row * per_rank, RB_DEV), jnp.int32),
            pltpu.SMEM((n_row * per_rank, columns), jnp.int32),
            pltpu.VMEM((CHUNKS // per_rank, size, block, block), a.dtype),
            pltpu.VMEM((block, columns * block), b.dtype),
            pltpu.VMEM((RB_DEV * block, columns * block), jnp.float32),
            pltpu.VMEM((n_col, 8, columns * block), jnp.float32),
            pltpu.VMEM((columns, RB_DEV, block, block), jnp.bfloat16),
            dma((3, n_row, CHUNKS)), dma((n_row, CHUNKS)),
            dma((2, n_col)), dma((2, n_col)), dma((2, n_row)), dma((2, n_row)), dma((n_col,)), dma((n_col,)),
            dma((8,)), dma((columns, RB_DEV)),
        ],
        compiler_params=pltpu.CompilerParams(
            collective_id=0, has_side_effects=True, vmem_limit_bytes=63 << 20),
        name="gather_multiply_normalize",
    )(a, b, matrix_rows, matrix_counts, slab_inner, slab_counts)


def solution(mesh):
    return jax.shard_map(
        functools.partial(on_device, mesh.shape["row"], mesh.shape["col"]),
        mesh=mesh,
        in_specs=(
            P("row", "col", None, None),
            P("row", "col"),
            P("row", "col"),
            P("row", "col", None, None),
            P("row", "col"),
            P("row"),
        ),
        out_specs=P("row", "col", None, None),
        check_vma=False,
    )
```

```python
import functools

import jax
import jax.numpy as jnp
from jax import lax
from jax.experimental import pallas as pl
from jax.experimental.pallas import tpu as pltpu
from jax.sharding import PartitionSpec as P

RB_DEV = 8
MESH = pl.DeviceIdType.MESH
CHUNKS = 6
PLAIN = CHUNKS - 1
UP, DOWN, SIDE = 0, 1, 2


def step_kernel(n_row, n_col, shape, a_ref, b_ref, rows_ref, counts_ref, inner_ref, slab_counts, out_ref,
                a_all, b_all, rows_all, counts_all, inner_all, rows_s, counts_s, inner_s,
                slot_s, source_s, stage, right, acc, sums_all, result,
                send, recv, b_send, b_recv, m_send, m_recv, s_send, s_recv, local, done):
    columns, slots, per_rank, capacity, block = shape
    each = CHUNKS // per_rank
    size = capacity // each
    n_z = n_row // 2
    r = lax.axis_index("row")
    c = lax.axis_index("col")
    z = lax.div(r, 2)
    y = lax.rem(r, 2)
    other = 1 - y
    beside = 2 * z + other
    has_up = z < n_z - 1
    has_down = z > 0

    barrier = pltpu.get_barrier_semaphore()
    for d in range(1, n_row):
        pl.semaphore_signal(barrier, inc=1, device_id={"row": lax.rem(r + d, n_row)}, device_id_type=MESH)
    for d in range(1, n_col):
        pl.semaphore_signal(barrier, inc=1, device_id={"col": lax.rem(c + d, n_col)}, device_id_type=MESH)
    pl.semaphore_wait(barrier, n_row + n_col - 2)

    def chunk(way, rank, ch, own=False):
        target = {UP: r + 2, DOWN: r - 2, SIDE: beside}[way]
        src = a_ref.at[ch] if own else a_all.at[rank, ch]
        return pltpu.make_async_remote_copy(
            src_ref=src, dst_ref=a_all.at[rank, ch], send_sem=send.at[way, rank, ch],
            recv_sem=recv.at[rank, ch], device_id={"row": target}, device_id_type=MESH)

    def arrived(rank, ch):
        pltpu.make_async_remote_copy(
            src_ref=a_all.at[rank, ch], dst_ref=a_all.at[rank, ch], send_sem=send.at[SIDE, rank, ch],
            recv_sem=recv.at[rank, ch], device_id={"row": beside}, device_id_type=MESH).wait_recv()

    def small(d):
        target = {"row": lax.rem(r + d, n_row)}
        return [
            pltpu.make_async_remote_copy(
                src_ref=src, dst_ref=dst.at[r], send_sem=m_send.at[n, d], recv_sem=m_recv.at[n, d],
                device_id=target, device_id_type=MESH)
            for n, (src, dst) in enumerate(((rows_ref, rows_all), (counts_ref, counts_all)))
        ]

    def slab(d):
        target = {"col": lax.rem(c + d, n_col)}
        return [
            pltpu.make_async_remote_copy(
                src_ref=inner_ref, dst_ref=inner_all.at[c], send_sem=b_send.at[1, d], recv_sem=b_recv.at[1, d],
                device_id=target, device_id_type=MESH),
            pltpu.make_async_remote_copy(
                src_ref=b_ref, dst_ref=b_all.at[c], send_sem=b_send.at[0, d], recv_sem=b_recv.at[0, d],
                device_id=target, device_id_type=MESH),
        ]

    def share(d):
        return pltpu.make_async_remote_copy(
            src_ref=sums_all.at[c], dst_ref=sums_all.at[c], send_sem=s_send.at[d], recv_sem=s_recv.at[d],
            device_id={"col": lax.rem(c + d, n_col)}, device_id_type=MESH)

    for ch in [PLAIN] + list(range(PLAIN)):
        chunk(SIDE, r, ch, True).start()
    for ch in range(CHUNKS):
        @pl.when(has_up)
        def _():
            chunk(UP, r, ch, True).start()

        @pl.when(has_down)
        def _():
            chunk(DOWN, r, ch, True).start()

    for d in range(1, n_row):
        for copy in small(d):
            copy.start()
    for d in range(1, n_col):
        for copy in slab(d):
            copy.start()
    mine = (
        pltpu.make_async_copy(a_ref, a_all.at[r], local.at[0]),
        pltpu.make_async_copy(b_ref, b_all.at[c], local.at[1]),
        pltpu.make_async_copy(rows_ref, rows_all.at[r], local.at[2]),
        pltpu.make_async_copy(counts_ref, counts_all.at[r], local.at[3]),
        pltpu.make_async_copy(inner_ref, inner_all.at[c], local.at[4]),
    )
    for copy in mine:
        copy.start()
    acc[...] = jnp.zeros_like(acc)

    arrived(beside, PLAIN)

    @pl.when(has_up)
    def _():
        chunk(UP, beside, PLAIN).start()

    @pl.when(has_down)
    def _():
        chunk(DOWN, beside, PLAIN).start()

    steps = [(0, ch, True) for ch in range(PLAIN)] + [(0, PLAIN, False), (1, PLAIN, False)]

    def sides(d, work):
        def one(side, carry):
            at = z + d * (2 * side - 1)

            @pl.when((at >= 0) & (at < n_z))
            def _():
                work(at)
            return carry

        lax.fori_loop(0, 2, one, 0)

    def relay(d, extra):
        for n, (flip, ch, cross) in enumerate(steps):
            column = other if flip else y

            @pl.when(z >= d)
            def _():
                rank = 2 * (z - d) + column
                arrived(rank, ch)

                @pl.when(has_up)
                def _():
                    chunk(UP, rank, ch).start()

                if cross:
                    chunk(SIDE, rank, ch).start()

            @pl.when(z + d < n_z)
            def _():
                rank = 2 * (z + d) + column
                arrived(rank, ch)

                @pl.when(has_down)
                def _():
                    chunk(DOWN, rank, ch).start()

                if cross:
                    chunk(SIDE, rank, ch).start()

            for work in extra.get(n, ()):
                work()

    def half(rank, kk):
        k = rank * per_rank + kk
        copy = pltpu.make_async_copy(a_all.at[rank, pl.ds(kk * each, each)], stage, local.at[0])
        copy.start()
        for j in range(columns):
            q = source_s[k, j]
            at = jnp.maximum(q, 0)
            value = b_all[lax.div(at, slots), j * slots + lax.rem(at, slots)]
            right[:, j * block:(j + 1) * block] = jnp.where(q >= 0, value, jnp.zeros_like(value))
        copy.wait()

        def block_row(i, carry):
            t = slot_s[k, i]
            at = jnp.maximum(t, 0)
            value = stage[lax.div(at, size), lax.rem(at, size)]
            left = jnp.where(t >= 0, value, jnp.zeros_like(value))
            rows = pl.ds(pl.multiple_of(i * block, block), block)
            acc[rows, :] += jnp.dot(left, right[...], preferred_element_type=jnp.float32)
            return carry

        lax.fori_loop(0, RB_DEV, block_row, 0, unroll=2)

    def whole(rank):
        def one(kk, carry):
            half(rank, kk)
            return carry

        lax.fori_loop(0, per_rank, one, 0)

    def await_side(rank, first, end):
        for ch in range(first, end):
            arrived(rank, ch)

    def own_whole(at):
        whole(2 * at + y)

    def side_whole(at):
        await_side(2 * at + other, 0, PLAIN)
        whole(2 * at + other)

    def own_half(kk):
        def work(at):
            half(2 * at + y, kk)
        return work

    def side_half(kk):
        def work(at):
            await_side(2 * at + other, kk * each, min(kk * each + each, PLAIN))
            half(2 * at + other, kk)
        return work

    relay(1, {})

    def complete():
        for copy in mine:
            copy.wait()
        for d in range(1, n_row):
            for copy in small(d):
                copy.wait()
        for d in range(1, n_col):
            for copy in slab(d):
                copy.wait()
        for n, (src, dst) in enumerate(((rows_all, rows_s), (counts_all, counts_s), (inner_all, inner_s))):
            copy = pltpu.make_async_copy(src, dst, local.at[5 + n])
            copy.start()
            copy.wait()
        lax.fori_loop(0, n_row, table, 0)

    def table(rank, carry):
        for kk in range(per_rank):
            k = rank * per_rank + kk
            for j in range(columns):
                q = jnp.int32(-1)
                for n in range(n_col * slots):
                    found = (inner_s[n // slots, j, n % slots] == k) & (n < slab_counts[j])
                    q = jnp.where(found, n, q)
                source_s[k, j] = q
            for i in range(RB_DEV):
                t = jnp.int32(-1)
                for n in range(capacity):
                    found = (rows_s[rank, kk, n] == i) & (n < counts_s[rank, 0, kk])
                    t = jnp.where(found, n, t)
                slot_s[k, i] = t
        return carry

    def side_here():
        await_side(beside, 0, PLAIN)
        whole(beside)

    relay(2, {
        0: (complete,),
        1: (lambda: whole(r),),
        2: (side_here,),
        3: (lambda: sides(1, own_whole),),
    })
    sides(1, side_whole)
    sides(2, own_whole)

    def later(d, carry):
        relay(d, {})
        sides(d - 1, side_whole)
        sides(d, own_whole)
        return carry

    lax.fori_loop(3, n_z - 1, later, 0)
    far = n_z - 1

    def side_halves(at):
        side_half(0)(at)
        side_half(1)(at)

    relay(far, {
        each - 1: (lambda: sides(far, own_half(0)), lambda: sides(far - 1, side_halves)),
        CHUNKS - 1: (lambda: sides(far, own_half(1)), lambda: sides(far, side_half(0))),
        CHUNKS: (lambda: sides(far, side_half(1)),),
    })

    def square(i, total):
        rows = pl.ds(pl.multiple_of(i * block, block), block)
        value = acc[rows, :]
        value = value * value
        return total + jnp.sum(value.reshape(block // 8, 8, columns * block), axis=0)

    total = lax.fori_loop(0, RB_DEV, square, jnp.zeros((8, columns * block), jnp.float32))
    sums_all[c] = total
    for d in range(1, n_col):
        share(d).start()

    for ch in range(CHUNKS):
        chunk(SIDE, r, ch, True).wait_send()

        @pl.when(has_up)
        def _():
            chunk(UP, r, ch, True).wait_send()

        @pl.when(has_down)
        def _():
            chunk(DOWN, r, ch, True).wait_send()

    @pl.when(has_up)
    def _():
        chunk(UP, beside, PLAIN).wait_send()

    @pl.when(has_down)
    def _():
        chunk(DOWN, beside, PLAIN).wait_send()

    def drain(d, carry):
        for flip, ch, cross in steps:
            column = other if flip else y

            @pl.when(z >= d)
            def _():
                rank = 2 * (z - d) + column

                @pl.when(has_up)
                def _():
                    chunk(UP, rank, ch).wait_send()

                if cross:
                    chunk(SIDE, rank, ch).wait_send()

            @pl.when(z + d < n_z)
            def _():
                rank = 2 * (z + d) + column

                @pl.when(has_down)
                def _():
                    chunk(DOWN, rank, ch).wait_send()

                if cross:
                    chunk(SIDE, rank, ch).wait_send()
        return carry

    lax.fori_loop(1, n_z, drain, 0)

    for d in range(1, n_col):
        share(d).wait()
    sums = jnp.sum(jnp.sum(sums_all[...], axis=0), axis=0, keepdims=True)
    factor = float(RB_DEV * n_col * block) / sums

    def scale(i, carry):
        rows = pl.ds(pl.multiple_of(i * block, block), block)
        value = acc[rows, :]
        value = (value * value * factor).astype(jnp.bfloat16)
        for j in range(columns):
            result[j, i] = value[:, j * block:(j + 1) * block]
            pltpu.make_async_copy(result.at[j, i], out_ref.at[j, i], done.at[j, i]).start()
        return carry

    lax.fori_loop(0, RB_DEV, scale, 0)

    def finish(i, carry):
        for j in range(columns):
            pltpu.make_async_copy(result.at[j, i], out_ref.at[j, i], done.at[j, i]).wait()
        return carry

    lax.fori_loop(0, RB_DEV, finish, 0)


def on_device(n_row, n_col, matrix_blocks, matrix_rows, matrix_counts, slab_blocks, slab_inner, slab_counts):
    per_rank, capacity, block = matrix_blocks.shape[0], matrix_blocks.shape[1], matrix_blocks.shape[2]
    columns, slots = slab_blocks.shape[0], slab_blocks.shape[1]
    held = per_rank * capacity
    size = held // CHUNKS
    a = matrix_blocks.reshape(CHUNKS, size, block, block)
    b = slab_blocks.reshape(columns * slots, block, block)
    matrix_counts = matrix_counts.reshape(1, per_rank)
    hbm = pl.BlockSpec(memory_space=pltpu.HBM)
    dma = pltpu.SemaphoreType.DMA
    rows_shape, counts_shape, inner_shape = (
        (n_row,) + matrix_rows.shape, (n_row,) + matrix_counts.shape, (n_col,) + slab_inner.shape)
    return pl.pallas_call(
        functools.partial(step_kernel, n_row, n_col, (columns, slots, per_rank, capacity, block)),
        out_shape=jax.ShapeDtypeStruct((columns, RB_DEV, block, block), jnp.bfloat16),
        in_specs=[hbm, hbm, hbm, hbm, hbm, pl.BlockSpec(memory_space=pltpu.SMEM)],
        out_specs=hbm,
        scratch_shapes=[
            pltpu.VMEM((n_row,) + a.shape, a.dtype),
            pltpu.VMEM((n_col,) + b.shape, b.dtype),
            pltpu.VMEM(rows_shape, jnp.int32),
            pltpu.VMEM(counts_shape, jnp.int32),
            pltpu.VMEM(inner_shape, jnp.int32),
            pltpu.SMEM(rows_shape, jnp.int32),
            pltpu.SMEM(counts_shape, jnp.int32),
            pltpu.SMEM(inner_shape, jnp.int32),
            pltpu.SMEM((n_row * per_rank, RB_DEV), jnp.int32),
            pltpu.SMEM((n_row * per_rank, columns), jnp.int32),
            pltpu.VMEM((CHUNKS // per_rank, size, block, block), a.dtype),
            pltpu.VMEM((block, columns * block), b.dtype),
            pltpu.VMEM((RB_DEV * block, columns * block), jnp.float32),
            pltpu.VMEM((n_col, 8, columns * block), jnp.float32),
            pltpu.VMEM((columns, RB_DEV, block, block), jnp.bfloat16),
            dma((3, n_row, CHUNKS)), dma((n_row, CHUNKS)),
            dma((2, n_col)), dma((2, n_col)), dma((2, n_row)), dma((2, n_row)), dma((n_col,)), dma((n_col,)),
            dma((8,)), dma((columns, RB_DEV)),
        ],
        compiler_params=pltpu.CompilerParams(
            collective_id=0, has_side_effects=True, vmem_limit_bytes=63 << 20),
        name="gather_multiply_normalize",
    )(a, b, matrix_rows, matrix_counts, slab_inner, slab_counts)


def solution(mesh):
    return jax.shard_map(
        functools.partial(on_device, mesh.shape["row"], mesh.shape["col"]),
        mesh=mesh,
        in_specs=(
            P("row", "col", None, None),
            P("row", "col"),
            P("row", "col"),
            P("row", "col", None, None),
            P("row", "col"),
            P("row"),
        ),
        out_specs=P("row", "col", None, None),
        check_vma=False,
    )
```
